256 devices in a mesh: segment: 8 (over z), space: 32 (over y, x, core).
Axes of the slice: x: 4, y: 4, z: 8, core: 2. Of those that a mesh axis runs over, the one named last changes fastest.
Arguments:
- video: bfloat16 [4, 2, 128, 24, 256], P(None, None, 'space'), may hold values from -6 to 6
- spatial_weight: bfloat16 [8, 2, 2, 2304, 256], P('segment'), may hold values from -0.125 to 0.125
- temporal_weight: bfloat16 [8, 2, 2, 768, 256], P('segment'), may hold values from -0.21875 to 0.21875
- section_blocks: int32 [8], P('segment'), may hold values from 1 to 2, as said below
Outputs:
- section_out: bfloat16 [8, 4, 2, 128, 24, 256], P('segment', None, None, 'space')
The draws below stay inside these ranges and needn't reach their ends.
Inputs may be any that keep to these rules, and one draw needn't show every extreme that they name: `section_blocks`: some section runs 2 blocks.
All inputs are finite; a program needn't handle non-finite values.
Results may differ from the reference program's by a relative error of at most 0.038.
Values may be sent and summed in bfloat16 or wider, within the bound.
No kernel may reach another device: no remote copies, remote signals or barrier semaphores. Data moves between devices by JAX's collectives and lax.ppermute only.
A program may use at most 64 MiB of HBM per device.

```python
import jax
import jax.numpy as jnp

C = 256
BLOCKS_MAX = 2
FRAMES = 2
COLS = 24
MICRO = 4
SEGMENTS = 8
ROWS = 128


def draw_section_blocks(key, part):
    first_key, second_key = jax.random.split(jax.random.fold_in(key, 11))
    counts = jax.random.randint(first_key, (SEGMENTS,), 1, BLOCKS_MAX + 1)
    chosen = jax.random.randint(second_key, (), 0, SEGMENTS)
    return counts.at[chosen].set(BLOCKS_MAX).astype(jnp.int32)


def levels(stream_key, extent, cuts, smallest, high):
    def one(position, parts):
        draws = jax.random.uniform(jax.random.fold_in(jax.random.fold_in(stream_key, 6), position), (parts,), jnp.float32, smallest / len(cuts), high / len(cuts))
        return jnp.repeat(jnp.exp(draws), extent[position] // parts).reshape((-1,) + (1,) * (len(extent) - position - 1))

    level = one(*cuts[0])
    for cut in cuts[1:]:
        level = level * one(*cut)
    return level


def centred(rng, extent, scale, limit, cuts=(), dtype=jnp.bfloat16):
    drawn = scale * jax.random.normal(rng, extent, jnp.float32)
    if cuts:
        drawn = drawn * levels(rng, extent, cuts, -0.22, 0.18)
    return jnp.clip(drawn, -limit, limit).astype(dtype)


def setup_inputs(seed: int = 0) -> dict:
    key_list = jax.random.split(jax.random.key(seed), 5)
    return {
        "video": centred(key_list[0], (MICRO, FRAMES, ROWS, COLS, C), 1.0, 6.0, ((2, 32),)),
        "spatial_weight": centred(key_list[1], (SEGMENTS, BLOCKS_MAX, 2, 9 * C, C), (9 * C) ** -0.5, 0.125, ((0, 8),)),
        "temporal_weight": centred(key_list[2], (SEGMENTS, BLOCKS_MAX, 2, 3 * C, C), (3 * C) ** -0.5, 0.21875, ((0, 8),)),
        "section_blocks": draw_section_blocks(jax.random.fold_in(key_list[4], 71), 0),
    }


def spatial_conv(active, weight):
    rows = active.shape[1]
    columns = active.shape[2]
    channels = active.shape[3]
    padded = jnp.pad(active, ((0, 0), (1, 1), (1, 1), (0, 0)))
    pieces = [padded[:, row_tap:row_tap + rows, col_tap:col_tap + columns] for row_tap in range(3) for col_tap in range(3)]
    stacked = jnp.concatenate(pieces, -1)
    summed = jnp.dot(stacked.reshape(-1, 9 * channels), weight, preferred_element_type=jnp.float32)
    return summed.reshape(active.shape)


def temporal_conv(stream, weight):
    frames = stream.shape[0]
    channels = stream.shape[3]
    joined = jnp.concatenate([stream[:1], stream[:1], stream], 0)
    stacked = jnp.concatenate([joined[0:frames], joined[1:frames + 1], joined[2:frames + 2]], -1)
    summed = jnp.dot(stacked.reshape(-1, 3 * channels), weight, preferred_element_type=jnp.float32)
    return summed.reshape(stream.shape)


def residual_block(state, ws_one, wt_one, ws_two, wt_two):
    active = jax.nn.silu(state.astype(jnp.float32)).astype(jnp.bfloat16)
    first_out = spatial_conv(active, ws_one).astype(jnp.bfloat16)
    hidden = jax.nn.silu(temporal_conv(first_out, wt_one)).astype(jnp.bfloat16)
    second_out = spatial_conv(hidden, ws_two).astype(jnp.bfloat16)
    return (state.astype(jnp.float32) + temporal_conv(second_out, wt_two)).astype(jnp.bfloat16)


def reference(video, spatial_weight, temporal_weight, section_blocks):
    state = video.reshape(MICRO * FRAMES, ROWS, COLS, C)
    results = []
    for section in range(SEGMENTS):
        for block in range(BLOCKS_MAX):
            updated = residual_block(state, spatial_weight[section, block, 0], temporal_weight[section, block, 0], spatial_weight[section, block, 1], temporal_weight[section, block, 1])
            state = jnp.where(block < section_blocks[section], updated, state)
        results.append(state.reshape(MICRO, FRAMES, ROWS, COLS, C))
    return jnp.stack(results)
```

```python
import jax
import jax.numpy as jnp
from jax import lax
from jax.experimental import pallas as pl
from jax.experimental.pallas import tpu as pltpu
from jax.sharding import PartitionSpec as P

C = 256
COLS = 24
OWN = 4
BF = jnp.bfloat16
F32 = jnp.float32


def silu(v):
    half = 0.5 * v
    return half * jnp.tanh(half) + half


def rows_of(flat):
    return flat.reshape(flat.shape[0] // COLS, COLS, C)


def spread(a):
    col = lax.broadcasted_iota(jnp.int32, (1, COLS, C), 1)
    left = jnp.where(col != 0, rows_of(pltpu.roll(a, 1, 0)), 0.0)
    right = jnp.where(col != COLS - 1, rows_of(pltpu.roll(a, a.shape[0] - 1, 0)), 0.0)
    return left.reshape(a.shape), a, right.reshape(a.shape)


def spatial(frames, w):
    tokens = frames[0].shape[0] - 2 * COLS
    out = []
    for a in frames:
        taps = spread(a)
        even = [t.astype(BF) for t in taps]
        odd = [t[COLS : COLS + tokens].astype(BF) for t in taps]
        lhs = jnp.concatenate(
            [e[:tokens] for e in even] + odd + [e[2 * COLS : 2 * COLS + tokens] for e in even], 1
        )
        out.append(jnp.dot(lhs, w, preferred_element_type=F32).astype(BF))
    return out


def temporal(frames, refs, opening, w):
    cache_ref, new_ref = refs
    old = [jnp.where(opening, frames[0], cache_ref[i]) for i in range(2)]
    seq = old + list(frames)
    for i in range(2):
        new_ref[i] = seq[len(frames) + i]
    return [
        jnp.dot(jnp.concatenate(seq[i : i + 3], 1), w, preferred_element_type=F32)
        for i in range(len(frames))
    ]


def clear(flat, margin, above, below):
    cut = margin * COLS
    if not cut:
        return flat
    top, rest = flat[:cut], flat[cut:-cut]
    return jnp.concatenate(
        [jnp.where(above, top, 0.0), rest, jnp.where(below, flat[-cut:], 0.0)], 0
    )


def block(state, ws, wt, b, caches_one, caches_two, opening, margin, above, below):
    act = [silu(x.astype(F32)) for x in state]
    one = spatial(act, ws[0, b, 0])
    mixed = temporal(one, caches_one, opening, wt[0, b, 0])
    hidden = [clear(silu(m), margin - 1, above, below) for m in mixed]
    two = spatial(hidden, ws[0, b, 1])
    mixed = temporal(two, caches_two, opening, wt[0, b, 1])
    inner = mixed[0].shape[0]
    out = []
    for x, m in zip(state, mixed):
        y = x[2 * COLS : 2 * COLS + inner].astype(F32) + m
        out.append(clear(y, margin - 2, above, below).astype(BF))
    return out


def kernel(flags, up, mid, down, ws, wt, a0, b0, a1, b1, out, na0, nb0, na1, nb1):
    frames = mid.shape[0]
    live, opening, depth = flags[0] == 1, flags[1] == 1, flags[2]
    above, below = flags[3] == 1, flags[4] == 1

    def load(f, margin):
        cut = (OWN - margin) * COLS
        low = jnp.where(above, up[f, cut:].astype(F32), 0.0).astype(BF)
        high = jnp.where(below, down[f, : margin * COLS].astype(F32), 0.0).astype(BF)
        return jnp.concatenate([low, mid[f], high], 0)

    @pl.when(live & (depth == 2))
    def _():
        state = [load(f, 4) for f in range(frames)]
        state = block(state, ws, wt, 0, (a0, na0), (b0, nb0), opening, 4, above, below)
        state = block(state, ws, wt, 1, (a1, na1), (b1, nb1), opening, 2, above, below)
        for f in range(frames):
            out[f] = state[f]

    @pl.when(live & (depth == 1))
    def _():
        state = [load(f, 2) for f in range(frames)]
        state = block(state, ws, wt, 0, (a1, na1), (b1, nb1), opening, 2, above, below)
        for f in range(frames):
            out[f] = state[f]


def section_step(frames):
    own = OWN * COLS
    shapes = [(2, (2 * OWN + 2) * COLS, C), (2, 2 * OWN * COLS, C), (2, (OWN + 2) * COLS, C), (2, own, C)]
    vm = pl.BlockSpec(memory_space=pltpu.VMEM)
    call = pl.pallas_call(
        kernel,
        in_specs=[pl.BlockSpec(memory_space=pltpu.SMEM)] + [vm] * 9,
        out_specs=[vm] * 5,
        out_shape=[jax.ShapeDtypeStruct(s, BF) for s in [(frames, own, C)] + shapes],
        compiler_params=pltpu.CompilerParams(vmem_limit_bytes=20 << 20),
        name="section_step",
    )
    return call, [jnp.zeros(s, BF) for s in shapes]


def ring(segments, spaces, shift):
    return [
        (k * spaces + s, (k + 1) % segments * spaces + (s + shift) % spaces)
        for k in range(segments)
        for s in range(spaces)
    ]


def per_device(video, spatial_weight, temporal_weight, section_blocks):
    groups, frames, rows, columns, channels = video.shape
    segments, spaces = lax.axis_size("segment"), lax.axis_size("space")
    place, lane = lax.axis_index("segment"), lax.axis_index("space")
    axes = ("segment", "space")
    video = video.reshape(groups, frames, rows * columns, channels)
    step, caches = section_step(frames)
    above, below = (lane > 0).astype(jnp.int32), (lane < spaces - 1).astype(jnp.int32)
    last = place == segments - 1

    def send(value):
        return [lax.ppermute(value, axes, ring(segments, spaces, d)) for d in (1, 0, -1)]

    arrived = send(video[0])
    stored = jnp.zeros(video.shape, BF)
    steps = segments + groups - 1
    for t in range(steps):
        group = t - place
        live = (group >= 0) & (group < groups)
        flags = jnp.stack(
            [live.astype(jnp.int32), (group == 0).astype(jnp.int32), section_blocks[0], above, below]
        )
        out, *caches = step(flags, *arrived, spatial_weight, temporal_weight, *caches)
        if t < steps - 1:
            value = jnp.where(last, video[t + 1], out) if t + 1 < groups else out
            arrived = send(value)
        slot = jnp.clip(group, 0, groups - 1)
        kept = lax.dynamic_index_in_dim(stored, slot, 0, keepdims=False)
        stored = lax.dynamic_update_index_in_dim(stored, jnp.where(live, out, kept), slot, 0)
    return stored.reshape(1, groups, frames, rows, columns, channels)


def solution(mesh):
    return jax.shard_map(
        per_device,
        mesh=mesh,
        in_specs=(
            P(None, None, "space", None, None),
            P("segment", None, None, None, None),
            P("segment", None, None, None, None),
            P("segment"),
        ),
        out_specs=P("segment", None, None, "space", None, None),
        check_vma=False,
    )
```

```python
import functools

import jax
import jax.numpy as jnp
from jax import lax
from jax.experimental import pallas as pl
from jax.experimental.pallas import tpu as pltpu
from jax.sharding import PartitionSpec as P

C = 256
COLS = 24
OWN = 4
BF = jnp.bfloat16
F32 = jnp.float32


def silu(v):
    half = 0.5 * v
    return half * jnp.tanh(half) + half


def rows_of(flat):
    return flat.reshape(flat.shape[0] // COLS, COLS, C)


def spread(a):
    col = lax.broadcasted_iota(jnp.int32, (1, COLS, C), 1)
    left = jnp.where(col != 0, rows_of(pltpu.roll(a, 1, 0)), 0.0)
    right = jnp.where(col != COLS - 1, rows_of(pltpu.roll(a, a.shape[0] - 1, 0)), 0.0)
    return left.reshape(a.shape), a, right.reshape(a.shape)


def spatial(frames, w):
    tokens = frames[0].shape[0] - 2 * COLS
    out = []
    for a in frames:
        taps = spread(a)
        even = [t.astype(BF) for t in taps]
        odd = [t[COLS : COLS + tokens].astype(BF) for t in taps]
        lhs = jnp.concatenate(
            [e[:tokens] for e in even] + odd + [e[2 * COLS : 2 * COLS + tokens] for e in even], 1
        )
        out.append(jnp.dot(lhs, w, preferred_element_type=F32).astype(BF))
    return out


def temporal(frames, refs, opening, w):
    cache_ref, new_ref = refs
    old = [jnp.where(opening, frames[0], cache_ref[i]) for i in range(2)]
    seq = old + list(frames)
    for i in range(2):
        new_ref[i] = seq[len(frames) + i]
    return [
        jnp.dot(jnp.concatenate(seq[i : i + 3], 1), w, preferred_element_type=F32)
        for i in range(len(frames))
    ]


def clear(flat, margin, above, below):
    cut = margin * COLS
    if not cut:
        return flat
    top, rest = flat[:cut], flat[cut:-cut]
    return jnp.concatenate(
        [jnp.where(above, top, 0.0), rest, jnp.where(below, flat[-cut:], 0.0)], 0
    )


def block(state, ws, wt, b, caches_one, caches_two, opening, margin, above, below):
    act = [silu(x.astype(F32)) for x in state]
    one = spatial(act, ws[0, b, 0])
    mixed = temporal(one, caches_one, opening, wt[0, b, 0])
    hidden = [clear(silu(m), margin - 1, above, below) for m in mixed]
    two = spatial(hidden, ws[0, b, 1])
    mixed = temporal(two, caches_two, opening, wt[0, b, 1])
    inner = mixed[0].shape[0]
    out = []
    for x, m in zip(state, mixed):
        y = x[2 * COLS : 2 * COLS + inner].astype(F32) + m
        out.append(clear(y, margin - 2, above, below).astype(BF))
    return out


def kernel(step, groups, facts, outer, mid, inner, ws, wt, a0, b0, a1, b1, out, na0, nb0, na1, nb1, between):
    frames = mid.shape[0]
    group = step - facts[0, 0]
    deep = facts[1, 0] == 2
    above, below, odd = facts[2, 0] == 1, facts[3, 0] == 1, facts[4, 0] == 1
    live, opening = (group >= 0) & (group < groups), group == 0

    def load(f, margin):
        part = margin * COLS
        rim = OWN * COLS - part
        low = jnp.where(odd, inner[f, rim:].astype(F32), outer[f, rim:].astype(F32))
        high = jnp.where(odd, outer[f, :part].astype(F32), inner[f, :part].astype(F32))
        low = jnp.where(above, low, 0.0).astype(BF)
        high = jnp.where(below, high, 0.0).astype(BF)
        return jnp.concatenate([low, mid[f], high], 0)

    @pl.when(live & deep)
    def _():
        state = [load(f, 4) for f in range(frames)]
        state = block(state, ws, wt, 0, (a0, na0), (b0, nb0), opening, 4, above, below)
        for f in range(frames):
            between[f] = state[f]

    @pl.when(live & ~deep)
    def _():
        for f in range(frames):
            between[f] = load(f, 2)

    @pl.when(live)
    def _():
        state = [between[f] for f in range(frames)]
        last = facts[1, 0] - 1
        state = block(state, ws, wt, last, (a1, na1), (b1, nb1), opening, 2, above, below)
        for f in range(frames):
            out[f] = state[f]


def load_weights(facts, ws_hbm, wt_hbm, ws, wt, a0, b0, a1, b1, sems):
    copies = [
        pltpu.make_async_copy(ws_hbm, ws, sems.at[0]), pltpu.make_async_copy(wt_hbm, wt, sems.at[1])
    ]
    for copy in copies:
        copy.start()
    for cache in (a0, b0, a1, b1):
        cache[...] = jnp.zeros_like(cache)
    for copy in copies:
        copy.wait()


def section_step(groups, frames, facts, ws, wt):
    own = OWN * COLS
    shapes = [(2, (2 * OWN + 2) * COLS, C), (2, 2 * OWN * COLS, C), (2, (OWN + 2) * COLS, C), (2, own, C)]
    shapes = [jax.ShapeDtypeStruct(s, BF) for s in shapes]
    vm = pl.BlockSpec(memory_space=pltpu.VMEM)
    params = pltpu.CompilerParams(vmem_limit_bytes=20 << 20)

    def step(t, *args):
        return pl.pallas_call(
            functools.partial(kernel, t, groups),
            in_specs=[vm] * 10,
            out_specs=[vm] * 5,
            out_shape=[jax.ShapeDtypeStruct((frames, own, C), BF)] + shapes,
            scratch_shapes=[pltpu.VMEM((frames, 2 * own, C), BF)],
            compiler_params=params,
            name="section_step",
        )(*args)

    ws, wt, *caches = pl.pallas_call(
        load_weights,
        in_specs=[vm] + [pl.BlockSpec(memory_space=pltpu.HBM)] * 2,
        out_specs=[vm] * 6,
        out_shape=[jax.ShapeDtypeStruct(w.shape, BF) for w in (ws, wt)] + shapes,
        scratch_shapes=[pltpu.SemaphoreType.DMA((2,))],
        compiler_params=params,
        name="load_weights",
    )(facts, *[pltpu.with_memory_space_constraint(w, pltpu.HBM) for w in (ws, wt)])
    return step, ws, wt, caches


def relay(value):
    def body(source, target):
        target[...] = source[...]

    vm = pl.BlockSpec(memory_space=pltpu.VMEM)
    return pl.pallas_call(
        body,
        in_specs=[vm],
        out_specs=vm,
        out_shape=jax.ShapeDtypeStruct(value.shape, value.dtype),
        cost_estimate=pl.CostEstimate(flops=0, transcendentals=0, bytes_accessed=2 * value.size * 2),
        compiler_params=pltpu.CompilerParams(vmem_limit_bytes=2 << 20),
        name="relay",
    )(value)


def moves(segments, spaces, hop, shift):
    return [
        (k * spaces + s, (k + hop) % segments * spaces + shift(s) % spaces)
        for k in range(segments)
        for s in range(spaces)
    ]


def across(s):
    return s + 1 if s % 2 else s - 1


def partner(s):
    return s ^ 1


def stay(s):
    return s


def per_device(video, spatial_weight, temporal_weight, section_blocks):
    groups, frames, rows, columns, channels = video.shape
    segments, spaces = lax.axis_size("segment"), lax.axis_size("space")
    place, lane = lax.axis_index("segment"), lax.axis_index("space")
    video = video.reshape(groups, frames, rows * columns, channels)
    steps = segments + groups - 1

    def move(value, hop, shift):
        return lax.ppermute(value, ("segment", "space"), moves(segments, spaces, hop, shift))

    mid = video[0]
    outer = move(mid, 0, across)
    inner = move(mid, 0, partner)
    facts = [place, section_blocks[0], lane > 0, lane < spaces - 1, lane % 2, 0, 0, 0]
    facts = jnp.broadcast_to(jnp.stack([jnp.int32(v) for v in facts])[:, None], (8, 128))
    order = [t - place for t in range(steps)]
    slots = [jnp.clip(group, 0, groups - 1) for group in order]
    lives = [(group >= 0) & (group < groups) for group in order]
    last = place == segments - 1
    facts, slots, lives, last, spatial_weight, temporal_weight = lax.optimization_barrier(
        (facts, slots, lives, last, spatial_weight, temporal_weight)
    )
    step, ws, wt, caches = section_step(groups, frames, facts, spatial_weight, temporal_weight)
    stored = jnp.zeros(video.shape, BF)
    for t in range(steps):
        out, *caches = step(t, facts, outer, mid, inner, ws, wt, *caches)
        if t < steps - 1:
            value = jnp.where(last, video[t + 1], out) if t + 1 < groups else out
            mid = move(value, 1, stay)
            inner = move(mid, 0, partner)
            outer = move(relay(value), 1, across)
        kept = lax.dynamic_index_in_dim(stored, slots[t], 0, keepdims=False)
        kept = jnp.where(lives[t], out, kept)
        stored = lax.dynamic_update_index_in_dim(stored, kept, slots[t], 0)
    return stored.reshape(1, groups, frames, rows, columns, channels)


def solution(mesh):
    return jax.shard_map(
        per_device,
        mesh=mesh,
        in_specs=(
            P(None, None, "space", None, None),
            P("segment", None, None, None, None),
            P("segment", None, None, None, None),
            P("segment"),
        ),
        out_specs=P("segment", None, None, "space", None, None),
        check_vma=False,
    )
```

```python
import functools

import jax
import jax.numpy as jnp
from jax import lax
from jax.experimental import pallas as pl
from jax.experimental.pallas import tpu as pltpu
from jax.sharding import PartitionSpec as P

C = 256
COLS = 24
OWN = 4
BF = jnp.bfloat16
F32 = jnp.float32


def silu(v):
    half = 0.5 * v
    return half * jnp.tanh(half) + half


def rows_of(flat):
    return flat.reshape(flat.shape[0] // COLS, COLS, C)


def spread(a):
    col = lax.broadcasted_iota(jnp.int32, (1, COLS, C), 1)
    left = jnp.where(col != 0, rows_of(pltpu.roll(a, 1, 0)), 0.0)
    right = jnp.where(col != COLS - 1, rows_of(pltpu.roll(a, a.shape[0] - 1, 0)), 0.0)
    return left.reshape(a.shape), a, right.reshape(a.shape)


def spatial(frames, w):
    tokens = frames[0].shape[0] - 2 * COLS
    taps = [
        jnp.concatenate([w[C * (3 * r + c) : C * (3 * r + c + 1)] for r in range(3)], 0) for c in range(3)
    ]
    col = lax.broadcasted_iota(jnp.int32, (1, COLS, C), 1)
    out = []
    for a in frames:
        even, odd = a.astype(BF), a[COLS : COLS + tokens].astype(BF)
        lhs = jnp.concatenate([even[:tokens], odd, even[2 * COLS : 2 * COLS + tokens]], 1)
        left, total, right = [jnp.dot(lhs, t, preferred_element_type=F32) for t in taps]
        left = jnp.where(col != 0, rows_of(pltpu.roll(left, 1, 0)), 0.0)
        right = jnp.where(col != COLS - 1, rows_of(pltpu.roll(right, tokens - 1, 0)), 0.0)
        total = rows_of(total) + left + right
        out.append(total.reshape(tokens, C).astype(BF))
    return out


def temporal(frames, refs, opening, w):
    cache_ref, new_ref = refs
    old = [jnp.where(opening, frames[0], cache_ref[i]) for i in range(2)]
    seq = old + list(frames)
    for i in range(2):
        new_ref[i] = seq[len(frames) + i]
    return [
        jnp.dot(jnp.concatenate(seq[i : i + 3], 1), w, preferred_element_type=F32)
        for i in range(len(frames))
    ]


def clear(flat, margin, above, below):
    cut = margin * COLS
    if not cut:
        return flat
    top, rest = flat[:cut], flat[cut:-cut]
    return jnp.concatenate(
        [jnp.where(above, top, 0.0), rest, jnp.where(below, flat[-cut:], 0.0)], 0
    )


def block(state, ws, wt, b, caches_one, caches_two, opening, margin, above, below):
    act = [silu(x.astype(F32)) for x in state]
    one = spatial(act, ws[0, b, 0])
    mixed = temporal(one, caches_one, opening, wt[0, b, 0])
    hidden = [clear(silu(m), margin - 1, above, below) for m in mixed]
    two = spatial(hidden, ws[0, b, 1])
    mixed = temporal(two, caches_two, opening, wt[0, b, 1])
    inner = mixed[0].shape[0]
    out = []
    for x, m in zip(state, mixed):
        y = x[2 * COLS : 2 * COLS + inner].astype(F32) + m
        out.append(clear(y, margin - 2, above, below).astype(BF))
    return out


def kernel(step, groups, facts, outer, mid, inner, ws, wt, a0, b0, a1, b1, out, na0, nb0, na1, nb1, between):
    frames = mid.shape[0]
    group = step - facts[0, 0]
    deep = facts[1, 0] == 2
    above, below, odd = facts[2, 0] == 1, facts[3, 0] == 1, facts[4, 0] == 1
    live, opening = (group >= 0) & (group < groups), group == 0

    def load(f, margin):
        part = margin * COLS
        rim = OWN * COLS - part
        low = jnp.where(odd, inner[f, rim:].astype(F32), outer[f, rim:].astype(F32))
        high = jnp.where(odd, outer[f, :part].astype(F32), inner[f, :part].astype(F32))
        low = jnp.where(above, low, 0.0).astype(BF)
        high = jnp.where(below, high, 0.0).astype(BF)
        return jnp.concatenate([low, mid[f], high], 0)

    @pl.when(live & deep)
    def _():
        state = [load(f, 4) for f in range(frames)]
        state = block(state, ws, wt, 0, (a0, na0), (b0, nb0), opening, 4, above, below)
        for f in range(frames):
            between[f] = state[f]

    @pl.when(live & ~deep)
    def _():
        for f in range(frames):
            between[f] = load(f, 2)

    @pl.when(live)
    def _():
        state = [between[f] for f in range(frames)]
        last = facts[1, 0] - 1
        state = block(state, ws, wt, last, (a1, na1), (b1, nb1), opening, 2, above, below)
        for f in range(frames):
            out[f] = state[f]


def load_weights(facts, ws_hbm, wt_hbm, ws, wt, a0, b0, a1, b1, sems):
    copies = [
        pltpu.make_async_copy(ws_hbm, ws, sems.at[0]), pltpu.make_async_copy(wt_hbm, wt, sems.at[1])
    ]
    for copy in copies:
        copy.start()
    for cache in (a0, b0, a1, b1):
        cache[...] = jnp.zeros_like(cache)
    for copy in copies:
        copy.wait()


def section_step(groups, frames, facts, ws, wt):
    own = OWN * COLS
    shapes = [(2, (2 * OWN + 2) * COLS, C), (2, 2 * OWN * COLS, C), (2, (OWN + 2) * COLS, C), (2, own, C)]
    shapes = [jax.ShapeDtypeStruct(s, BF) for s in shapes]
    vm = pl.BlockSpec(memory_space=pltpu.VMEM)
    params = pltpu.CompilerParams(vmem_limit_bytes=20 << 20)

    def step(t, *args):
        return pl.pallas_call(
            functools.partial(kernel, t, groups),
            in_specs=[vm] * 10,
            out_specs=[vm] * 5,
            out_shape=[jax.ShapeDtypeStruct((frames, own, C), BF)] + shapes,
            scratch_shapes=[pltpu.VMEM((frames, 2 * own, C), BF)],
            compiler_params=params,
            name="section_step",
        )(*args)

    ws, wt, *caches = pl.pallas_call(
        load_weights,
        in_specs=[vm] + [pl.BlockSpec(memory_space=pltpu.HBM)] * 2,
        out_specs=[vm] * 6,
        out_shape=[jax.ShapeDtypeStruct(w.shape, BF) for w in (ws, wt)] + shapes,
        scratch_shapes=[pltpu.SemaphoreType.DMA((2,))],
        compiler_params=params,
        name="load_weights",
    )(facts, *[pltpu.with_memory_space_constraint(w, pltpu.HBM) for w in (ws, wt)])
    return step, ws, wt, caches


def relay(value):
    def body(source, target):
        target[...] = source[...]

    vm = pl.BlockSpec(memory_space=pltpu.VMEM)
    return pl.pallas_call(
        body,
        in_specs=[vm],
        out_specs=vm,
        out_shape=jax.ShapeDtypeStruct(value.shape, value.dtype),
        cost_estimate=pl.CostEstimate(flops=0, transcendentals=0, bytes_accessed=2 * value.size * 2),
        compiler_params=pltpu.CompilerParams(vmem_limit_bytes=2 << 20),
        name="relay",
    )(value)


def moves(segments, spaces, hop, shift):
    return [
        (k * spaces + s, (k + hop) % segments * spaces + shift(s) % spaces)
        for k in range(segments)
        for s in range(spaces)
    ]


def across(s):
    return s + 1 if s % 2 else s - 1


def partner(s):
    return s ^ 1


def stay(s):
    return s


def per_device(video, spatial_weight, temporal_weight, section_blocks):
    groups, frames, rows, columns, channels = video.shape
    segments, spaces = lax.axis_size("segment"), lax.axis_size("space")
    place, lane = lax.axis_index("segment"), lax.axis_index("space")
    video = video.reshape(groups, frames, rows * columns, channels)
    steps = segments + groups - 1

    def move(value, hop, shift):
        return lax.ppermute(value, ("segment", "space"), moves(segments, spaces, hop, shift))

    mid = video[0]
    outer = move(mid, 0, across)
    inner = move(mid, 0, partner)
    facts = [place, section_blocks[0], lane > 0, lane < spaces - 1, lane % 2, 0, 0, 0]
    facts = jnp.broadcast_to(jnp.stack([jnp.int32(v) for v in facts])[:, None], (8, 128))
    order = [t - place for t in range(steps)]
    slots = [jnp.clip(group, 0, groups - 1) for group in order]
    lives = [(group >= 0) & (group < groups) for group in order]
    last = place == segments - 1
    facts, slots, lives, last, spatial_weight, temporal_weight = lax.optimization_barrier(
        (facts, slots, lives, last, spatial_weight, temporal_weight)
    )
    step, ws, wt, caches = section_step(groups, frames, facts, spatial_weight, temporal_weight)
    stored = jnp.zeros(video.shape, BF)
    for t in range(steps):
        out, *caches = step(t, facts, outer, mid, inner, ws, wt, *caches)
        if t < steps - 1:
            value = jnp.where(last, video[t + 1], out) if t + 1 < groups else out
            mid = move(value, 1, stay)
            inner = move(mid, 0, partner)
            outer = move(relay(value), 1, across)
        kept = lax.dynamic_index_in_dim(stored, slots[t], 0, keepdims=False)
        kept = jnp.where(lives[t], out, kept)
        stored = lax.dynamic_update_index_in_dim(stored, kept, slots[t], 0)
    return stored.reshape(1, groups, frames, rows, columns, channels)


def solution(mesh):
    return jax.shard_map(
        per_device,
        mesh=mesh,
        in_specs=(
            P(None, None, "space", None, None),
            P("segment", None, None, None, None),
            P("segment", None, None, None, None),
            P("segment"),
        ),
        out_specs=P("segment", None, None, "space", None, None),
        check_vma=False,
    )
```

```python
import functools

import jax
import jax.numpy as jnp
from jax import lax
from jax.experimental import pallas as pl
from jax.experimental.pallas import tpu as pltpu
from jax.sharding import PartitionSpec as P

C = 256
COLS = 24
OWN = 4
BF = jnp.bfloat16
F32 = jnp.float32


def silu(v):
    half = 0.5 * v
    return half * jnp.tanh(half) + half


def rows_of(flat):
    return flat.reshape(flat.shape[0] // COLS, COLS, C)


def spread(a):
    col = lax.broadcasted_iota(jnp.int32, (1, COLS, C), 1)
    left = jnp.where(col != 0, rows_of(pltpu.roll(a, 1, 0)), 0.0)
    right = jnp.where(col != COLS - 1, rows_of(pltpu.roll(a, a.shape[0] - 1, 0)), 0.0)
    return left.reshape(a.shape), a, right.reshape(a.shape)


def spatial(frames, w):
    tokens = frames[0].shape[0] - 2 * COLS
    taps = [
        jnp.concatenate([w[C * (3 * r + c) : C * (3 * r + c + 1)] for r in range(3)], 0) for c in range(3)
    ]
    col = lax.broadcasted_iota(jnp.int32, (1, COLS, C), 1)
    out = []
    for a in frames:
        even, odd = a.astype(BF), a[COLS : COLS + tokens].astype(BF)
        lhs = jnp.concatenate([even[:tokens], odd, even[2 * COLS : 2 * COLS + tokens]], 1)
        left, total, right = [jnp.dot(lhs, t, preferred_element_type=F32) for t in taps]
        left = jnp.where(col != 0, rows_of(pltpu.roll(left, 1, 0)), 0.0)
        right = jnp.where(col != COLS - 1, rows_of(pltpu.roll(right, tokens - 1, 0)), 0.0)
        total = rows_of(total) + left + right
        out.append(total.reshape(tokens, C).astype(BF))
    return out


def temporal(frames, refs, opening, w):
    cache_ref, new_ref = refs
    old = [jnp.where(opening, frames[0], cache_ref[i]) for i in range(2)]
    seq = old + list(frames)
    for i in range(2):
        new_ref[i] = seq[len(frames) + i]
    return [
        jnp.dot(jnp.concatenate(seq[i : i + 3], 1), w, preferred_element_type=F32)
        for i in range(len(frames))
    ]


def clear(flat, margin, above, below):
    cut = margin * COLS
    if not cut:
        return flat
    top, rest = flat[:cut], flat[cut:-cut]
    return jnp.concatenate(
        [jnp.where(above, top, 0.0), rest, jnp.where(below, flat[-cut:], 0.0)], 0
    )


def block(state, one, ws, wt, b, caches_one, caches_two, opening, margin, above, below):
    mixed = temporal(one, caches_one, opening, wt[0, b, 0])
    hidden = [clear(silu(m), margin - 1, above, below) for m in mixed]
    two = spatial(hidden, ws[0, b, 1])
    mixed = temporal(two, caches_two, opening, wt[0, b, 1])
    inner = mixed[0].shape[0]
    out = []
    for x, m in zip(state, mixed):
        y = x[2 * COLS : 2 * COLS + inner].astype(F32) + m
        out.append(clear(y, margin - 2, above, below).astype(BF))
    return out


def first_spatial(state, w):
    return spatial([silu(x.astype(F32)) for x in state], w)


def early(step, groups, facts, mid, inner, ws, near):
    group = step - facts[0, 0]
    odd = facts[4, 0] == 1

    @pl.when((group >= 0) & (group < groups) & (facts[1, 0] == 2))
    def _():
        state = []
        for f in range(mid.shape[0]):
            own, other = mid[f].astype(F32), inner[f].astype(F32)
            low, high = jnp.where(odd, other, own), jnp.where(odd, own, other)
            state.append(jnp.concatenate([low, high], 0).astype(BF))
        for f, rows in enumerate(first_spatial(state, ws[0, 0, 0])):
            near[f] = rows


def kernel(step, groups, facts, near, outer, mid, inner, ws, wt, a0, b0, a1, b1, out, na0, nb0, na1, nb1, between):
    frames = mid.shape[0]
    group = step - facts[0, 0]
    deep = facts[1, 0] == 2
    above, below, odd = facts[2, 0] == 1, facts[3, 0] == 1, facts[4, 0] == 1
    live, opening = (group >= 0) & (group < groups), group == 0

    def load(f, margin):
        part = margin * COLS
        rim = OWN * COLS - part
        low = jnp.where(odd, inner[f, rim:].astype(F32), outer[f, rim:].astype(F32))
        high = jnp.where(odd, outer[f, :part].astype(F32), inner[f, :part].astype(F32))
        low = jnp.where(above, low, 0.0).astype(BF)
        high = jnp.where(below, high, 0.0).astype(BF)
        return jnp.concatenate([low, mid[f], high], 0)

    @pl.when(live & deep)
    def _():
        state = [load(f, 4) for f in range(frames)]
        cut = 6 * COLS
        rest = [jnp.where(odd, x[cut:].astype(F32), x[:cut].astype(F32)).astype(BF) for x in state]
        one = []
        for f, far in enumerate(first_spatial(rest, ws[0, 0, 0])):
            far, known = far.astype(F32), near[f].astype(F32)
            up, down = jnp.concatenate([far, known], 0), jnp.concatenate([known, far], 0)
            one.append(jnp.where(odd, down, up).astype(BF))
        state = block(state, one, ws, wt, 0, (a0, na0), (b0, nb0), opening, 4, above, below)
        for f in range(frames):
            between[f] = state[f]

    @pl.when(live & ~deep)
    def _():
        for f in range(frames):
            between[f] = load(f, 2)

    @pl.when(live)
    def _():
        state = [between[f] for f in range(frames)]
        last = facts[1, 0] - 1
        one = first_spatial(state, ws[0, last, 0])
        state = block(state, one, ws, wt, last, (a1, na1), (b1, nb1), opening, 2, above, below)
        for f in range(frames):
            out[f] = state[f]


def load_weights(facts, ws_hbm, wt_hbm, ws, wt, a0, b0, a1, b1, sems):
    copies = [
        pltpu.make_async_copy(ws_hbm, ws, sems.at[0]), pltpu.make_async_copy(wt_hbm, wt, sems.at[1])
    ]
    for copy in copies:
        copy.start()
    for cache in (a0, b0, a1, b1):
        cache[...] = jnp.zeros_like(cache)
    for copy in copies:
        copy.wait()


def section_step(groups, frames, facts, ws, wt):
    own = OWN * COLS
    shapes = [(2, (2 * OWN + 2) * COLS, C), (2, 2 * OWN * COLS, C), (2, (OWN + 2) * COLS, C), (2, own, C)]
    shapes = [jax.ShapeDtypeStruct(s, BF) for s in shapes]
    vm = pl.BlockSpec(memory_space=pltpu.VMEM)
    params = pltpu.CompilerParams(vmem_limit_bytes=20 << 20)

    def step(t, facts, outer, mid, inner, ws, *args):
        near = pl.pallas_call(
            functools.partial(early, t, groups),
            in_specs=[vm] * 4,
            out_specs=vm,
            out_shape=jax.ShapeDtypeStruct((frames, 6 * COLS, C), BF),
            compiler_params=params,
            name="early_rows",
        )(facts, mid, inner, ws)
        return pl.pallas_call(
            functools.partial(kernel, t, groups),
            in_specs=[vm] * 11,
            out_specs=[vm] * 5,
            out_shape=[jax.ShapeDtypeStruct((frames, own, C), BF)] + shapes,
            scratch_shapes=[pltpu.VMEM((frames, 2 * own, C), BF)],
            compiler_params=params,
            name="section_step",
        )(facts, near, outer, mid, inner, ws, *args)

    ws, wt, *caches = pl.pallas_call(
        load_weights,
        in_specs=[vm] + [pl.BlockSpec(memory_space=pltpu.HBM)] * 2,
        out_specs=[vm] * 6,
        out_shape=[jax.ShapeDtypeStruct(w.shape, BF) for w in (ws, wt)] + shapes,
        scratch_shapes=[pltpu.SemaphoreType.DMA((2,))],
        compiler_params=params,
        name="load_weights",
    )(facts, *[pltpu.with_memory_space_constraint(w, pltpu.HBM) for w in (ws, wt)])
    return step, ws, wt, caches


def relay(value):
    def body(source, target):
        target[...] = source[...]

    vm = pl.BlockSpec(memory_space=pltpu.VMEM)
    return pl.pallas_call(
        body,
        in_specs=[vm],
        out_specs=vm,
        out_shape=jax.ShapeDtypeStruct(value.shape, value.dtype),
        cost_estimate=pl.CostEstimate(flops=0, transcendentals=0, bytes_accessed=2 * value.size * 2),
        compiler_params=pltpu.CompilerParams(vmem_limit_bytes=2 << 20),
        name="relay",
    )(value)


def moves(segments, spaces, hop, shift):
    return [
        (k * spaces + s, (k + hop) % segments * spaces + shift(s) % spaces)
        for k in range(segments)
        for s in range(spaces)
    ]


def across(s):
    return s + 1 if s % 2 else s - 1


def partner(s):
    return s ^ 1


def stay(s):
    return s


def per_device(video, spatial_weight, temporal_weight, section_blocks):
    groups, frames, rows, columns, channels = video.shape
    segments, spaces = lax.axis_size("segment"), lax.axis_size("space")
    place, lane = lax.axis_index("segment"), lax.axis_index("space")
    video = video.reshape(groups, frames, rows * columns, channels)
    steps = segments + groups - 1

    def move(value, hop, shift):
        return lax.ppermute(value, ("segment", "space"), moves(segments, spaces, hop, shift))

    mid = video[0]
    outer = move(mid, 0, across)
    inner = move(mid, 0, partner)
    facts = [place, section_blocks[0], lane > 0, lane < spaces - 1, lane % 2, 0, 0, 0]
    facts = jnp.broadcast_to(jnp.stack([jnp.int32(v) for v in facts])[:, None], (8, 128))
    order = [t - place for t in range(steps)]
    slots = [jnp.clip(group, 0, groups - 1) for group in order]
    lives = [(group >= 0) & (group < groups) for group in order]
    last = place == segments - 1
    facts, slots, lives, last, spatial_weight, temporal_weight = lax.optimization_barrier(
        (facts, slots, lives, last, spatial_weight, temporal_weight)
    )
    step, ws, wt, caches = section_step(groups, frames, facts, spatial_weight, temporal_weight)
    stored = jnp.zeros(video.shape, BF)
    for t in range(steps):
        out, *caches = step(t, facts, outer, mid, inner, ws, wt, *caches)
        if t < steps - 1:
            value = jnp.where(last, video[t + 1], out) if t + 1 < groups else out
            mid = move(value, 1, stay)
            inner = move(mid, 0, partner)
            outer = move(relay(value), 1, across)
        kept = lax.dynamic_index_in_dim(stored, slots[t], 0, keepdims=False)
        kept = jnp.where(lives[t], out, kept)
        stored = lax.dynamic_update_index_in_dim(stored, kept, slots[t], 0)
    return stored.reshape(1, groups, frames, rows, columns, channels)


def solution(mesh):
    return jax.shard_map(
        per_device,
        mesh=mesh,
        in_specs=(
            P(None, None, "space", None, None),
            P("segment", None, None, None, None),
            P("segment", None, None, None, None),
            P("segment"),
        ),
        out_specs=P("segment", None, None, "space", None, None),
        check_vma=False,
    )
```

```python
import functools

import jax
import jax.numpy as jnp
from jax import lax
from jax.experimental import pallas as pl
from jax.experimental.pallas import tpu as pltpu
from jax.sharding import PartitionSpec as P

C = 256
COLS = 24
OWN = 4
BF = jnp.bfloat16
F32 = jnp.float32


def silu(v):
    half = 0.5 * v
    return half * jnp.tanh(half) + half


def rows_of(flat):
    return flat.reshape(flat.shape[0] // COLS, COLS, C)


def spread(a):
    col = lax.broadcasted_iota(jnp.int32, (1, COLS, C), 1)
    left = jnp.where(col != 0, rows_of(pltpu.roll(a, 1, 0)), 0.0)
    right = jnp.where(col != COLS - 1, rows_of(pltpu.roll(a, a.shape[0] - 1, 0)), 0.0)
    return left.reshape(a.shape), a, right.reshape(a.shape)


def spatial(frames, w):
    tokens = frames[0].shape[0] - 2 * COLS
    taps = [
        jnp.concatenate([w[C * (3 * r + c) : C * (3 * r + c + 1)] for r in range(3)], 0) for c in range(3)
    ]
    col = lax.broadcasted_iota(jnp.int32, (1, COLS, C), 1)
    out = []
    for a in frames:
        even, odd = a.astype(BF), a[COLS : COLS + tokens].astype(BF)
        lhs = jnp.concatenate([even[:tokens], odd, even[2 * COLS : 2 * COLS + tokens]], 1)
        left, total, right = [jnp.dot(lhs, t, preferred_element_type=F32) for t in taps]
        left = jnp.where(col != 0, rows_of(pltpu.roll(left, 1, 0)), 0.0)
        right = jnp.where(col != COLS - 1, rows_of(pltpu.roll(right, tokens - 1, 0)), 0.0)
        total = rows_of(total) + left + right
        out.append(total.reshape(tokens, C).astype(BF))
    return out


def history(frames, old, opening):
    return [jnp.where(opening, frames[0], x) for x in old] + list(frames)


def temporal(seq, w):
    return [
        jnp.dot(jnp.concatenate(seq[i : i + 3], 1), w, preferred_element_type=F32)
        for i in range(len(seq) - 2)
    ]


def stream(frames, refs, opening):
    cache_ref, new_ref = refs
    seq = history(frames, [cache_ref[0], cache_ref[1]], opening)
    for i in range(2):
        new_ref[i] = seq[len(frames) + i]
    return seq


def clear(flat, margin, above, below):
    cut = margin * COLS
    if not cut:
        return flat
    top, rest = flat[:cut], flat[cut:-cut]
    return jnp.concatenate(
        [jnp.where(above, top, 0.0), rest, jnp.where(below, flat[-cut:], 0.0)], 0
    )


def block(state, one, ws, wt, b, caches_one, caches_two, opening, margin, above, below, silus=None):
    seq = stream(one, caches_one, opening)
    hidden = silus(seq) if silus else [silu(m) for m in temporal(seq, wt[0, b, 0])]
    hidden = [clear(h, margin - 1, above, below) for h in hidden]
    two = spatial(hidden, ws[0, b, 1])
    mixed = temporal(stream(two, caches_two, opening), wt[0, b, 1])
    inner = mixed[0].shape[0]
    out = []
    for x, m in zip(state, mixed):
        y = x[2 * COLS : 2 * COLS + inner].astype(F32) + m
        out.append(clear(y, margin - 2, above, below).astype(BF))
    return out


def first_spatial(state, w):
    return spatial([silu(x.astype(F32)) for x in state], w)


def early(step, groups, facts, mid, inner, ws, wt, a0, near, warm):
    group = step - facts[0, 0]
    odd = facts[4, 0] == 1

    @pl.when((group >= 0) & (group < groups) & (facts[1, 0] == 2))
    def _():
        state = []
        for f in range(mid.shape[0]):
            own, other = mid[f].astype(F32), inner[f].astype(F32)
            low, high = jnp.where(odd, other, own), jnp.where(odd, own, other)
            state.append(jnp.concatenate([low, high], 0).astype(BF))
        rows = first_spatial(state, ws[0, 0, 0])
        cut = 6 * COLS
        old = [jnp.where(odd, a0[i, :cut], a0[i, -cut:]) for i in range(2)]
        mixed = temporal(history(rows, old, group == 0), wt[0, 0, 0])
        for f in range(mid.shape[0]):
            near[f] = rows[f]
            warm[f] = silu(mixed[f]).astype(BF)


def kernel(step, groups, facts, near, warm, outer, mid, inner, ws, wt, a0, b0, a1, b1, out, na0, nb0, na1, nb1, between):
    frames = mid.shape[0]
    group = step - facts[0, 0]
    deep = facts[1, 0] == 2
    above, below, odd = facts[2, 0] == 1, facts[3, 0] == 1, facts[4, 0] == 1
    live, opening = (group >= 0) & (group < groups), group == 0

    def load(f, margin):
        part = margin * COLS
        rim = OWN * COLS - part
        low = jnp.where(odd, inner[f, rim:].astype(F32), outer[f, rim:].astype(F32))
        high = jnp.where(odd, outer[f, :part].astype(F32), inner[f, :part].astype(F32))
        low = jnp.where(above, low, 0.0).astype(BF)
        high = jnp.where(below, high, 0.0).astype(BF)
        return jnp.concatenate([low, mid[f], high], 0)

    @pl.when(live & deep)
    def _():
        state = [load(f, 4) for f in range(frames)]
        cut = 6 * COLS
        rest = [jnp.where(odd, x[cut:].astype(F32), x[:cut].astype(F32)).astype(BF) for x in state]

        def join(far, known):
            up, down = jnp.concatenate([far, known], 0), jnp.concatenate([known, far], 0)
            return jnp.where(odd, down, up)

        def silus(seq):
            far = temporal([jnp.where(odd, x[cut:], x[:-cut]) for x in seq], wt[0, 0, 0])
            return [join(silu(m), warm[f].astype(F32)) for f, m in enumerate(far)]

        far = first_spatial(rest, ws[0, 0, 0])
        one = [join(far[f].astype(F32), near[f].astype(F32)).astype(BF) for f in range(frames)]
        state = block(state, one, ws, wt, 0, (a0, na0), (b0, nb0), opening, 4, above, below, silus)
        for f in range(frames):
            between[f] = state[f]

    @pl.when(live & ~deep)
    def _():
        for f in range(frames):
            between[f] = load(f, 2)

    @pl.when(live)
    def _():
        state = [between[f] for f in range(frames)]
        last = facts[1, 0] - 1
        one = first_spatial(state, ws[0, last, 0])
        state = block(state, one, ws, wt, last, (a1, na1), (b1, nb1), opening, 2, above, below)
        for f in range(frames):
            out[f] = state[f]


def load_weights(facts, ws_hbm, wt_hbm, ws, wt, a0, b0, a1, b1, sems):
    copies = [
        pltpu.make_async_copy(ws_hbm, ws, sems.at[0]), pltpu.make_async_copy(wt_hbm, wt, sems.at[1])
    ]
    for copy in copies:
        copy.start()
    for cache in (a0, b0, a1, b1):
        cache[...] = jnp.zeros_like(cache)
    for copy in copies:
        copy.wait()


def section_step(groups, frames, facts, ws, wt):
    own = OWN * COLS
    shapes = [(2, (2 * OWN + 2) * COLS, C), (2, 2 * OWN * COLS, C), (2, (OWN + 2) * COLS, C), (2, own, C)]
    shapes = [jax.ShapeDtypeStruct(s, BF) for s in shapes]
    vm = pl.BlockSpec(memory_space=pltpu.VMEM)
    params = pltpu.CompilerParams(vmem_limit_bytes=20 << 20)

    def step(t, facts, outer, mid, inner, ws, wt, a0, *args):
        near, warm = pl.pallas_call(
            functools.partial(early, t, groups),
            in_specs=[vm] * 6,
            out_specs=[vm] * 2,
            out_shape=[jax.ShapeDtypeStruct((frames, 6 * COLS, C), BF)] * 2,
            compiler_params=params,
            name="early_rows",
        )(facts, mid, inner, ws, wt, a0)
        return pl.pallas_call(
            functools.partial(kernel, t, groups),
            in_specs=[vm] * 12,
            out_specs=[vm] * 5,
            out_shape=[jax.ShapeDtypeStruct((frames, own, C), BF)] + shapes,
            scratch_shapes=[pltpu.VMEM((frames, 2 * own, C), BF)],
            compiler_params=params,
            name="section_step",
        )(facts, near, warm, outer, mid, inner, ws, wt, a0, *args)

    ws, wt, *caches = pl.pallas_call(
        load_weights,
        in_specs=[vm] + [pl.BlockSpec(memory_space=pltpu.HBM)] * 2,
        out_specs=[vm] * 6,
        out_shape=[jax.ShapeDtypeStruct(w.shape, BF) for w in (ws, wt)] + shapes,
        scratch_shapes=[pltpu.SemaphoreType.DMA((2,))],
        compiler_params=params,
        name="load_weights",
    )(facts, *[pltpu.with_memory_space_constraint(w, pltpu.HBM) for w in (ws, wt)])
    return step, ws, wt, caches


def relay(value):
    def body(source, target):
        target[...] = source[...]

    vm = pl.BlockSpec(memory_space=pltpu.VMEM)
    return pl.pallas_call(
        body,
        in_specs=[vm],
        out_specs=vm,
        out_shape=jax.ShapeDtypeStruct(value.shape, value.dtype),
        cost_estimate=pl.CostEstimate(flops=0, transcendentals=0, bytes_accessed=2 * value.size * 2),
        compiler_params=pltpu.CompilerParams(vmem_limit_bytes=2 << 20),
        name="relay",
    )(value)


def moves(segments, spaces, hop, shift):
    return [
        (k * spaces + s, (k + hop) % segments * spaces + shift(s) % spaces)
        for k in range(segments)
        for s in range(spaces)
    ]


def across(s):
    return s + 1 if s % 2 else s - 1


def partner(s):
    return s ^ 1


def stay(s):
    return s


def per_device(video, spatial_weight, temporal_weight, section_blocks):
    groups, frames, rows, columns, channels = video.shape
    segments, spaces = lax.axis_size("segment"), lax.axis_size("space")
    place, lane = lax.axis_index("segment"), lax.axis_index("space")
    video = video.reshape(groups, frames, rows * columns, channels)
    steps = segments + groups - 1

    def move(value, hop, shift):
        return lax.ppermute(value, ("segment", "space"), moves(segments, spaces, hop, shift))

    mid = video[0]
    outer = move(mid, 0, across)
    inner = move(mid, 0, partner)
    facts = [place, section_blocks[0], lane > 0, lane < spaces - 1, lane % 2, 0, 0, 0]
    facts = jnp.broadcast_to(jnp.stack([jnp.int32(v) for v in facts])[:, None], (8, 128))
    order = [t - place for t in range(steps)]
    slots = [jnp.clip(group, 0, groups - 1) for group in order]
    lives = [(group >= 0) & (group < groups) for group in order]
    last = place == segments - 1
    facts, slots, lives, last, spatial_weight, temporal_weight = lax.optimization_barrier(
        (facts, slots, lives, last, spatial_weight, temporal_weight)
    )
    step, ws, wt, caches = section_step(groups, frames, facts, spatial_weight, temporal_weight)
    stored = jnp.zeros(video.shape, BF)
    for t in range(steps):
        out, *caches = step(t, facts, outer, mid, inner, ws, wt, *caches)
        if t < steps - 1:
            value = jnp.where(last, video[t + 1], out) if t + 1 < groups else out
            mid = move(value, 1, stay)
            inner = move(mid, 0, partner)
            outer = move(relay(value), 1, across)
        kept = lax.dynamic_index_in_dim(stored, slots[t], 0, keepdims=False)
        kept = jnp.where(lives[t], out, kept)
        stored = lax.dynamic_update_index_in_dim(stored, kept, slots[t], 0)
    return stored.reshape(1, groups, frames, rows, columns, channels)


def solution(mesh):
    return jax.shard_map(
        per_device,
        mesh=mesh,
        in_specs=(
            P(None, None, "space", None, None),
            P("segment", None, None, None, None),
            P("segment", None, None, None, None),
            P("segment"),
        ),
        out_specs=P("segment", None, None, "space", None, None),
        check_vma=False,
    )
```

```python
import functools

import jax
import jax.numpy as jnp
from jax import lax
from jax.experimental import pallas as pl
from jax.experimental.pallas import tpu as pltpu
from jax.sharding import PartitionSpec as P

C = 256
COLS = 24
OWN = 4
BF = jnp.bfloat16
F32 = jnp.float32


def silu(v):
    half = 0.5 * v
    return half * jnp.tanh(half) + half


def rows_of(flat):
    return flat.reshape(flat.shape[0] // COLS, COLS, C)


def spread(a):
    col = lax.broadcasted_iota(jnp.int32, (1, COLS, C), 1)
    left = jnp.where(col != 0, rows_of(pltpu.roll(a, 1, 0)), 0.0)
    right = jnp.where(col != COLS - 1, rows_of(pltpu.roll(a, a.shape[0] - 1, 0)), 0.0)
    return left.reshape(a.shape), a, right.reshape(a.shape)


def spatial(frames, w):
    tokens = frames[0].shape[0] - 2 * COLS
    taps = [
        jnp.concatenate([w[C * (3 * r + c) : C * (3 * r + c + 1)] for r in range(3)], 0) for c in range(3)
    ]
    col = lax.broadcasted_iota(jnp.int32, (1, COLS, C), 1)
    out = []
    for a in frames:
        even, odd = a.astype(BF), a[COLS : COLS + tokens].astype(BF)
        lhs = jnp.concatenate([even[:tokens], odd, even[2 * COLS : 2 * COLS + tokens]], 1)
        left, total, right = [jnp.dot(lhs, t, preferred_element_type=F32) for t in taps]
        left = jnp.where(col != 0, rows_of(pltpu.roll(left, 1, 0)), 0.0)
        right = jnp.where(col != COLS - 1, rows_of(pltpu.roll(right, tokens - 1, 0)), 0.0)
        total = rows_of(total) + left + right
        out.append(total.reshape(tokens, C).astype(BF))
    return out


def history(frames, old, opening):
    return [jnp.where(opening, frames[0], x) for x in old] + list(frames)


def temporal(seq, w):
    return [
        jnp.dot(jnp.concatenate(seq[i : i + 3], 1), w, preferred_element_type=F32)
        for i in range(len(seq) - 2)
    ]


def stream(frames, refs, opening):
    cache_ref, new_ref = refs
    seq = history(frames, [cache_ref[0], cache_ref[1]], opening)
    for i in range(2):
        new_ref[i] = seq[len(frames) + i]
    return seq


def clear(flat, margin, above, below):
    cut = margin * COLS
    if not cut:
        return flat
    top, rest = flat[:cut], flat[cut:-cut]
    return jnp.concatenate(
        [jnp.where(above, top, 0.0), rest, jnp.where(below, flat[-cut:], 0.0)], 0
    )


def block(state, one, ws, wt, b, caches_one, caches_two, opening, margin, above, below, silus=None):
    seq = stream(one, caches_one, opening)
    hidden = silus(seq) if silus else [silu(m) for m in temporal(seq, wt[0, b, 0])]
    hidden = [clear(h, margin - 1, above, below) for h in hidden]
    two = spatial(hidden, ws[0, b, 1])
    mixed = temporal(stream(two, caches_two, opening), wt[0, b, 1])
    inner = mixed[0].shape[0]
    out = []
    for x, m in zip(state, mixed):
        y = x[2 * COLS : 2 * COLS + inner].astype(F32) + m
        out.append(clear(y, margin - 2, above, below).astype(BF))
    return out


def first_spatial(state, w):
    return spatial([silu(x.astype(F32)) for x in state], w)


def early(step, groups, facts, mid, inner, ws, wt, a0, near, warm):
    group = step - facts[0, 0]
    odd = facts[4, 0] == 1

    @pl.when((group >= 0) & (group < groups) & (facts[1, 0] == 2))
    def _():
        state = []
        for f in range(mid.shape[0]):
            own, other = mid[f], inner[f]
            low, high = jnp.where(odd, other, own), jnp.where(odd, own, other)
            state.append(jnp.concatenate([low, high], 0))
        rows = first_spatial(state, ws[0, 0, 0])
        cut = 6 * COLS
        old = [jnp.where(odd, a0[i, :cut], a0[i, -cut:]) for i in range(2)]
        mixed = temporal(history(rows, old, group == 0), wt[0, 0, 0])
        for f in range(mid.shape[0]):
            near[f] = rows[f]
            warm[f] = silu(mixed[f]).astype(BF)


def kernel(step, groups, facts, near, warm, outer, mid, inner, ws, wt, a0, b0, a1, b1, out, na0, nb0, na1, nb1, between):
    frames = mid.shape[0]
    group = step - facts[0, 0]
    deep = facts[1, 0] == 2
    above, below, odd = facts[2, 0] == 1, facts[3, 0] == 1, facts[4, 0] == 1
    live, opening = (group >= 0) & (group < groups), group == 0

    def load(f, margin):
        part = margin * COLS
        rim = OWN * COLS - part
        low = jnp.where(odd, inner[f, rim:], outer[f, rim:])
        high = jnp.where(odd, outer[f, :part], inner[f, :part])
        low = jnp.where(above, low, jnp.zeros_like(low))
        high = jnp.where(below, high, jnp.zeros_like(high))
        return jnp.concatenate([low, mid[f], high], 0)

    @pl.when(live & deep)
    def _():
        state = [load(f, 4) for f in range(frames)]
        cut = 6 * COLS
        rest = [jnp.where(odd, x[cut:], x[:cut]) for x in state]

        def join(far, known):
            up, down = jnp.concatenate([far, known], 0), jnp.concatenate([known, far], 0)
            return jnp.where(odd, down, up)

        def silus(seq):
            far = temporal([jnp.where(odd, x[cut:], x[:-cut]) for x in seq], wt[0, 0, 0])
            return [join(silu(m), warm[f].astype(F32)) for f, m in enumerate(far)]

        far = first_spatial(rest, ws[0, 0, 0])
        one = [join(far[f], near[f]) for f in range(frames)]
        state = block(state, one, ws, wt, 0, (a0, na0), (b0, nb0), opening, 4, above, below, silus)
        for f in range(frames):
            between[f] = state[f]

    @pl.when(live & ~deep)
    def _():
        for f in range(frames):
            between[f] = load(f, 2)

    @pl.when(live)
    def _():
        state = [between[f] for f in range(frames)]
        last = facts[1, 0] - 1
        one = first_spatial(state, ws[0, last, 0])
        state = block(state, one, ws, wt, last, (a1, na1), (b1, nb1), opening, 2, above, below)
        for f in range(frames):
            out[f] = state[f]


def load_weights(facts, ws_hbm, wt_hbm, ws, wt, a0, b0, a1, b1, sems):
    copies = [
        pltpu.make_async_copy(ws_hbm, ws, sems.at[0]), pltpu.make_async_copy(wt_hbm, wt, sems.at[1])
    ]
    for copy in copies:
        copy.start()
    for cache in (a0, b0, a1, b1):
        cache[...] = jnp.zeros_like(cache)
    for copy in copies:
        copy.wait()


def section_step(groups, frames, facts, ws, wt):
    own = OWN * COLS
    shapes = [(2, (2 * OWN + 2) * COLS, C), (2, 2 * OWN * COLS, C), (2, (OWN + 2) * COLS, C), (2, own, C)]
    shapes = [jax.ShapeDtypeStruct(s, BF) for s in shapes]
    vm = pl.BlockSpec(memory_space=pltpu.VMEM)
    params = pltpu.CompilerParams(vmem_limit_bytes=20 << 20)

    def step(t, facts, outer, mid, inner, ws, wt, a0, *args):
        near, warm = pl.pallas_call(
            functools.partial(early, t, groups),
            in_specs=[vm] * 6,
            out_specs=[vm] * 2,
            out_shape=[jax.ShapeDtypeStruct((frames, 6 * COLS, C), BF)] * 2,
            compiler_params=params,
            name="early_rows",
        )(facts, mid, inner, ws, wt, a0)
        return pl.pallas_call(
            functools.partial(kernel, t, groups),
            in_specs=[vm] * 12,
            out_specs=[vm] * 5,
            out_shape=[jax.ShapeDtypeStruct((frames, own, C), BF)] + shapes,
            scratch_shapes=[pltpu.VMEM((frames, 2 * own, C), BF)],
            compiler_params=params,
            name="section_step",
        )(facts, near, warm, outer, mid, inner, ws, wt, a0, *args)

    ws, wt, *caches = pl.pallas_call(
        load_weights,
        in_specs=[vm] + [pl.BlockSpec(memory_space=pltpu.HBM)] * 2,
        out_specs=[vm] * 6,
        out_shape=[jax.ShapeDtypeStruct(w.shape, BF) for w in (ws, wt)] + shapes,
        scratch_shapes=[pltpu.SemaphoreType.DMA((2,))],
        compiler_params=params,
        name="load_weights",
    )(facts, *[pltpu.with_memory_space_constraint(w, pltpu.HBM) for w in (ws, wt)])
    return step, ws, wt, caches


def relay(value):
    def body(source, target):
        target[...] = source[...]

    vm = pl.BlockSpec(memory_space=pltpu.VMEM)
    return pl.pallas_call(
        body,
        in_specs=[vm],
        out_specs=vm,
        out_shape=jax.ShapeDtypeStruct(value.shape, value.dtype),
        cost_estimate=pl.CostEstimate(flops=0, transcendentals=0, bytes_accessed=2 * value.size * 2),
        compiler_params=pltpu.CompilerParams(vmem_limit_bytes=2 << 20),
        name="relay",
    )(value)


def moves(segments, spaces, hop, shift):
    return [
        (k * spaces + s, (k + hop) % segments * spaces + shift(s) % spaces)
        for k in range(segments)
        for s in range(spaces)
    ]


def across(s):
    return s + 1 if s % 2 else s - 1


def partner(s):
    return s ^ 1


def stay(s):
    return s


def per_device(video, spatial_weight, temporal_weight, section_blocks):
    groups, frames, rows, columns, channels = video.shape
    segments, spaces = lax.axis_size("segment"), lax.axis_size("space")
    place, lane = lax.axis_index("segment"), lax.axis_index("space")
    video = video.reshape(groups, frames, rows * columns, channels)
    steps = segments + groups - 1

    def move(value, hop, shift):
        return lax.ppermute(value, ("segment", "space"), moves(segments, spaces, hop, shift))

    mid = video[0]
    outer = move(mid, 0, across)
    inner = move(mid, 0, partner)
    facts = [place, section_blocks[0], lane > 0, lane < spaces - 1, lane % 2, 0, 0, 0]
    facts = jnp.broadcast_to(jnp.stack([jnp.int32(v) for v in facts])[:, None], (8, 128))
    order = [t - place for t in range(steps)]
    slots = [jnp.clip(group, 0, groups - 1) for group in order]
    lives = [(group >= 0) & (group < groups) for group in order]
    last = place == segments - 1
    facts, slots, lives, last, spatial_weight, temporal_weight = lax.optimization_barrier(
        (facts, slots, lives, last, spatial_weight, temporal_weight)
    )
    step, ws, wt, caches = section_step(groups, frames, facts, spatial_weight, temporal_weight)
    stored = jnp.zeros(video.shape, BF)
    for t in range(steps):
        out, *caches = step(t, facts, outer, mid, inner, ws, wt, *caches)
        if t < steps - 1:
            value = jnp.where(last, video[t + 1], out) if t + 1 < groups else out
            mid = move(value, 1, stay)
            inner = move(mid, 0, partner)
            outer = move(relay(value), 1, across)
        kept = lax.dynamic_index_in_dim(stored, slots[t], 0, keepdims=False)
        kept = jnp.where(lives[t], out, kept)
        stored = lax.dynamic_update_index_in_dim(stored, kept, slots[t], 0)
    return stored.reshape(1, groups, frames, rows, columns, channels)


def solution(mesh):
    return jax.shard_map(
        per_device,
        mesh=mesh,
        in_specs=(
            P(None, None, "space", None, None),
            P("segment", None, None, None, None),
            P("segment", None, None, None, None),
            P("segment"),
        ),
        out_specs=P("segment", None, None, "space", None, None),
        check_vma=False,
    )
```
